32 devices in a mesh: wide: 8 (over z, y), narrow: 4 (over x, core).
Axes of the slice: x: 2, y: 2, z: 4, core: 2. Of those that a mesh axis runs over, the one named last changes fastest.
Arguments:
- desc_a: bfloat16 [4096, 128], P('wide'), may hold values from -6 to 6
- desc_b: bfloat16 [32768, 128], P('narrow'), may hold values from -6 to 6
- logmass_a: float32 [4096], P('wide'), may hold values from -6 to 6
- logmass_b: float32 [32768], P('narrow'), may hold values from -6 to 6
- g_start: float32 [32768], P('narrow'), may hold values from -1 to 16, as said below
Outputs:
- potential_a: float32 [4096], P('wide')
- potential_b: float32 [32768], P('narrow')
- flow_a: float32 [4096, 128], P('wide')
- flow_b: float32 [32768, 128], P(('narrow', 'wide'))
The draws below stay inside these ranges and needn't reach their ends.
Inputs may be any that keep to these rules, and one draw needn't show every extreme that they name: `g_start`: potentials of view B carried over from the previous pair of views.
All inputs are finite; a program needn't handle non-finite values.
Results may differ from the reference program's by a relative error of at most 0.01.
Values may be sent and summed in bfloat16 or wider, within the bound.
A program may use at most 64 MiB of HBM per device.

```python
import math
import jax
import jax.numpy as jnp
from jax import lax

DIM = 128
ITERS = 2
NA = 4096
NB = 32768


def draw_g_start(key, part):
    third_key = jax.random.fold_in(key, 2)
    values = 0.3 * jax.random.normal(third_key, (NB,), jnp.float32)
    return jnp.clip(values, -1.0, 1.0)


def level_of(key, dims, shards, low, high):
    loudness = 1.0
    for position, parts in shards:
        draws = jax.random.uniform(jax.random.fold_in(jax.random.fold_in(key, 6), position), (parts,), jnp.float32, low / len(shards), high / len(shards))
        loudness = loudness * jnp.repeat(jnp.exp(draws), dims[position] // parts).reshape((-1,) + (1,) * (len(dims) - 1 - position))
    return loudness


def gaussian(stream_key, dims, width, most, cuts=(), dtype=jnp.bfloat16):
    factor_of = level_of(stream_key, dims, cuts, -0.22, 0.18) if cuts else 1.0
    values = jax.random.normal(stream_key, dims, jnp.float32) * width * factor_of
    return jnp.minimum(jnp.maximum(values, -most), most).astype(dtype)


def setup_inputs(seed: int = 0) -> dict:
    arg_keys = jax.random.split(jax.random.key(seed), 6)
    desc_a = gaussian(arg_keys[0], (NA, DIM), 1.0, 6.0, ((0, 8),))
    desc_b = gaussian(arg_keys[1], (NB, DIM), 1.0, 6.0, ((0, 4),))
    logmass_a = gaussian(arg_keys[2], (NA,), 2.0, 6.0, ((0, 8),), jnp.float32)
    logmass_b = gaussian(arg_keys[3], (NB,), 2.0, 6.0, ((0, 4),), jnp.float32)
    g_start = draw_g_start(jax.random.fold_in(arg_keys[5], 71), 0)
    return dict(desc_a=desc_a, desc_b=desc_b, logmass_a=logmass_a, logmass_b=logmass_b, g_start=g_start)


EPS = 0.05

def unit_rows(desc):
    wide32 = desc.astype(jnp.float32)
    return (wide32 / jnp.sqrt(lax.optimization_barrier(jnp.sum(wide32 * wide32, axis=1, keepdims=True)) + 1e-06)).astype(jnp.bfloat16)

def cost_of(left, right):
    return 2.0 - 2.0 * jnp.dot(left, right.T, preferred_element_type=jnp.float32)

def reference(desc_a, desc_b, logmass_a, logmass_b, g_start):
    unit_a = unit_rows(desc_a)
    unit_b = unit_rows(desc_b)
    n_tokens = unit_a.shape[0]
    feat_width = unit_a.shape[1]
    row_step = math.gcd(n_tokens, 512)
    a_tiles = unit_a.reshape(-1, row_step, feat_width)

    def row_lse(potential):

        def one_tile(tile_a):
            scores = (potential[None, :] - cost_of(tile_a, unit_b)) / EPS
            highest = lax.optimization_barrier(jnp.max(scores, axis=1))
            return highest + jnp.log(lax.optimization_barrier(jnp.sum(jnp.exp(scores - highest[:, None]), axis=1)))
        return lax.map(one_tile, a_tiles).reshape(-1)

    def col_lse(row_pot):

        def one_tile(state_now, inputs):
            highest, summed = state_now
            tile_a, row_part = inputs
            scores = (row_part[:, None] - cost_of(tile_a, unit_b)) / EPS
            new_high = jnp.maximum(highest, lax.optimization_barrier(jnp.max(scores, axis=0)))
            summed = summed * jnp.exp(highest - new_high) + lax.optimization_barrier(jnp.sum(jnp.exp(scores - new_high[None, :]), axis=0))
            return ((new_high, summed), None)
        init = (jnp.full((unit_b.shape[0],), -jnp.inf, jnp.float32), jnp.zeros((unit_b.shape[0],), jnp.float32))
        (highest, summed), _ = lax.scan(one_tile, init, (a_tiles, row_pot.reshape(-1, row_step)))
        return highest + jnp.log(summed)
    potential_b = g_start
    for sweep_index in range(ITERS):
        row_pot = EPS * logmass_a - EPS * row_lse(potential_b)
        lse_b = col_lse(row_pot)
        potential_b = EPS * logmass_b - EPS * lse_b

    def add_flow(state_now, inputs):
        tile_a, row_part = inputs
        weights = jnp.exp((row_part[:, None] - cost_of(tile_a, unit_b)) / EPS - lse_b[None, :]).astype(jnp.bfloat16)
        return (state_now + jnp.dot(weights.T, tile_a, preferred_element_type=jnp.float32), None)
    sums_b, _ = lax.scan(add_flow, jnp.zeros((unit_b.shape[0], feat_width), jnp.float32), (a_tiles, row_pot.reshape(-1, row_step)))
    flow_b = sums_b - unit_b.astype(jnp.float32)
    lse_a = row_lse(potential_b)
    potential_a = EPS * logmass_a - EPS * lse_a

    def flow_tile(inputs):
        tile_a, lse_part = inputs
        weights = jnp.exp((potential_b[None, :] - cost_of(tile_a, unit_b)) / EPS - lse_part[:, None]).astype(jnp.bfloat16)
        return jnp.dot(weights, unit_b, preferred_element_type=jnp.float32) - tile_a.astype(jnp.float32)
    flow_a = lax.map(flow_tile, (a_tiles, lse_a.reshape(-1, row_step))).reshape(n_tokens, feat_width)
    return (potential_a, potential_b, flow_a, flow_b)
```

```python
import functools

import jax
import jax.numpy as jnp
from jax import lax
from jax.experimental import pallas as pl
from jax.experimental.pallas import tpu as pltpu
from jax.sharding import PartitionSpec as P

ITERS = 2
EPS = 0.05
SHIFT = 30.0
CENTRE = 2.0 / EPS
MESH = pl.DeviceIdType.MESH
NT = (((1,), (1,)), ((), ()))


def unit_of(desc):
    wide32 = desc.astype(jnp.float32)
    total = jnp.sum(wide32 * wide32, axis=1, keepdims=True) + 1e-06
    return (wide32 / jnp.sqrt(total)).astype(jnp.bfloat16)


def scaled_rows(logs, top):
    val = jnp.exp(logs - top + SHIFT)
    high = val.astype(jnp.bfloat16).astype(jnp.float32)
    low = val - high
    row = lax.broadcasted_iota(jnp.int32, (16, logs.shape[1]), 0)
    return val, jnp.where(row == 0, high, jnp.where(row == 1, low, 0.0)).astype(jnp.bfloat16)


def kernel(
    nw, nn,
    desc_a, desc_b, lm_a, lm_b, g_start,
    pot_a, pot_b, flow_a, flow_b,
    a_in, unit_a, unit_b, a_t, b_t, k_rows, k_cols, rows16, weighted,
    phi_in, psi_in, lse_in, flow_in, l_row, t_row, fsum,
    a_send, a_recv, phi_send, phi_recv, psi_send, psi_recv, lse_send, lse_recv, f_send, f_recv,
):
    wide = lax.axis_index("wide")
    narrow = lax.axis_index("narrow")
    rows, feat = desc_a.shape
    cols = desc_b.shape[0]
    share = cols // nw
    all_rows = nw * rows
    own_cols = pl.ds(pl.multiple_of(wide * share, share), share)
    own_rows = pl.ds(pl.multiple_of(wide * rows, rows), rows)

    barrier = pltpu.get_barrier_semaphore()
    for k in range(1, nw):
        pl.semaphore_signal(
            barrier, inc=1, device_id={"wide": lax.rem(wide + k, nw)}, device_id_type=MESH
        )
    for k in range(1, nn):
        pl.semaphore_signal(
            barrier, inc=1, device_id={"narrow": lax.rem(narrow + k, nn)}, device_id_type=MESH
        )

    def spread(axis, size, me, src, dst, send, recv):
        copies = []
        for k in range(1, size):
            copy = pltpu.make_async_remote_copy(
                src_ref=src, dst_ref=dst, send_sem=send.at[k], recv_sem=recv.at[k],
                device_id={axis: lax.rem(me + k, size)}, device_id_type=MESH,
            )
            copy.start()
            copies.append(copy)
        return copies

    def finish(copies):
        for copy in copies:
            copy.wait()

    own_unit = unit_of(desc_a[...])
    step_b = min(cols, 512)

    @pl.loop(0, cols // step_b)
    def _(c):
        at = pl.ds(pl.multiple_of(c * step_b, step_b), step_b)
        unit_b[at, :] = unit_of(desc_b[at, :])

    pl.semaphore_wait(barrier, nw + nn - 2)
    a_copies = spread("wide", nw, wide, desc_a, a_in.at[wide], a_send, a_recv)

    chunk = 256

    @pl.loop(0, cols // chunk)
    def _(c):
        at = pl.ds(pl.multiple_of(c * chunk, chunk), chunk)
        dots = lax.dot_general(unit_b[at, :], own_unit, NT, preferred_element_type=jnp.float32)
        k_cols[at, :] = jnp.exp(dots * CENTRE).astype(jnp.bfloat16)

    def log_sums(logs, mat, out):
        top = jnp.max(logs, axis=1, keepdims=True)
        val, pair = scaled_rows(logs, top)
        depth, width = mat.shape
        rows16[:, :depth] = pair
        block = min(width, 256)
        for c in range(width // block):
            at = pl.ds(c * block, block)
            got = jnp.dot(rows16[:, :depth], mat[:, at], preferred_element_type=jnp.float32)
            out[:, at] = jnp.log(got[0:1, :] + got[1:2, :]) + (top - SHIFT - CENTRE)
        return val, top

    def weighted_sums(val, tokens_t, mat, base, top, write):
        depth, width = mat.shape
        step = min(depth, 1024)
        for c in range(depth // step):
            at = pl.ds(c * step, step)
            part = tokens_t[:, at].astype(jnp.float32) * val[:, c * step:(c + 1) * step]
            weighted[:, at] = part.astype(jnp.bfloat16)
        block = min(width, 256)
        for c in range(width // block):
            at = pl.ds(c * block, block)
            got = jnp.dot(weighted[:, :depth], mat[:, at], preferred_element_type=jnp.float32)
            scale = jnp.exp((top - SHIFT - CENTRE) - base[:, at])
            write(at, got * scale)

    def joined(buf, t, n):
        return jnp.concatenate([buf[t, w] for w in range(n)], axis=1)

    def narrow_lse(t):
        parts = [lse_in[t, n] for n in range(nn)]
        top = functools.reduce(jnp.maximum, parts)
        return top + jnp.log(sum(jnp.exp(p - top) for p in parts))

    pending = []
    psi = g_start[...] / EPS
    for t in range(ITERS + 1):
        v_val, v_top = log_sums(psi, k_cols, l_row)
        lse_in[t, narrow] = l_row[...]
        lse_copies = spread(
            "narrow", nn, narrow, lse_in.at[t, narrow], lse_in.at[t, narrow],
            lse_send.at[t], lse_recv.at[t],
        )
        if t == ITERS:
            def put_a(at, value):
                flow_in[narrow, :, at] = value.astype(jnp.bfloat16)

            weighted_sums(v_val, b_t, k_cols, l_row, v_top, put_a)
            f_copies = spread(
                "narrow", nn, narrow, flow_in.at[narrow], flow_in.at[narrow], f_send, f_recv
            )
            finish(lse_copies)
            lse_a = narrow_lse(t)
            pot_a[...] = EPS * (lm_a[...] - lse_a)
            finish(f_copies)
            acc = jnp.zeros((feat, rows), jnp.float32)
            for n in range(nn):
                acc += flow_in[n].astype(jnp.float32) * jnp.exp(lse_in[t, n] - lse_a)
            flow_a[...] = acc.T - own_unit.astype(jnp.float32)
            break
        finish(lse_copies)
        phi_in[t, wide] = lm_a[...] - narrow_lse(t)
        phi_copies = spread(
            "wide", nw, wide, phi_in.at[t, wide], phi_in.at[t, wide],
            phi_send.at[t], phi_recv.at[t],
        )
        if t == 0:
            finish(a_copies)
            a_in[wide] = desc_a[...]

            for w in range(nw):
                unit_a[pl.ds(w * rows, rows), :] = unit_of(a_in[w])
            own_b = unit_b[own_cols, :]

            @pl.loop(0, all_rows // chunk)
            def _(c):
                at = pl.ds(pl.multiple_of(c * chunk, chunk), chunk)
                dots = lax.dot_general(unit_a[at, :], own_b, NT, preferred_element_type=jnp.float32)
                k_rows[at, :] = jnp.exp(dots * CENTRE).astype(jnp.bfloat16)

        finish(phi_copies)
        phi = joined(phi_in, t, nw)
        u_val, u_top = log_sums(phi, k_rows, t_row)
        psi_in[t, wide] = lm_b[:, own_cols] - t_row[...]
        psi_copies = spread(
            "wide", nw, wide, psi_in.at[t, wide], psi_in.at[t, wide],
            psi_send.at[t], psi_recv.at[t],
        )
        if t == 0:
            @pl.loop(0, cols // step_b)
            def _(c):
                at = pl.ds(pl.multiple_of(c * step_b, step_b), step_b)
                b_t[:, at] = unit_b[at, :].T

            for w in range(nw):
                at = pl.ds(w * rows, rows)
                a_t[:, at] = unit_a[at, :].T
        if t == ITERS - 1:
            def put_b(at, value):
                flow_b[at, :] = value.T - unit_b[
                    pl.ds(pl.multiple_of(wide * share + at.start, 128), at.size), :
                ].astype(jnp.float32)

            weighted_sums(u_val, a_t, k_rows, t_row, u_top, put_b)
        finish(psi_copies)
        psi = joined(psi_in, t, nw)
    pot_b[...] = EPS * psi


def on_device(desc_a, desc_b, logmass_a, logmass_b, g_start):
    nw = lax.axis_size("wide")
    nn = lax.axis_size("narrow")
    rows, feat = desc_a.shape
    cols = desc_b.shape[0]
    share = cols // nw
    all_rows = nw * rows
    longest = max(all_rows, cols)
    f32, bf16 = jnp.float32, jnp.bfloat16
    vmem = pltpu.VMEM
    dma = pltpu.SemaphoreType.DMA
    outs = pl.pallas_call(
        functools.partial(kernel, nw, nn),
        out_shape=(
            jax.ShapeDtypeStruct((1, rows), f32),
            jax.ShapeDtypeStruct((1, cols), f32),
            jax.ShapeDtypeStruct((rows, feat), f32),
            jax.ShapeDtypeStruct((share, feat), f32),
        ),
        in_specs=[pl.BlockSpec(memory_space=vmem)] * 5,
        out_specs=(pl.BlockSpec(memory_space=vmem),) * 4,
        scratch_shapes=[
            vmem((nw, rows, feat), bf16),
            vmem((all_rows, feat), bf16),
            vmem((cols, feat), bf16),
            vmem((feat, all_rows), bf16),
            vmem((feat, cols), bf16),
            vmem((all_rows, share), bf16),
            vmem((cols, rows), bf16),
            vmem((16, longest), bf16),
            vmem((feat, longest), bf16),
            vmem((ITERS, nw, 1, rows), f32),
            vmem((ITERS, nw, 1, share), f32),
            vmem((ITERS + 1, nn, 1, rows), f32),
            vmem((nn, feat, rows), bf16),
            vmem((1, rows), f32),
            vmem((1, share), f32),
            vmem((8, 128), f32),
            dma((nw,)), dma((nw,)),
            dma((ITERS, nw)), dma((ITERS, nw)),
            dma((ITERS, nw)), dma((ITERS, nw)),
            dma((ITERS + 1, nn)), dma((ITERS + 1, nn)),
            dma((nn,)), dma((nn,)),
        ],
        compiler_params=pltpu.CompilerParams(
            collective_id=0, has_side_effects=True, vmem_limit_bytes=60 * 1024 * 1024
        ),
        name="sinkhorn",
    )(
        desc_a, desc_b, logmass_a.reshape(1, rows), logmass_b.reshape(1, cols),
        g_start.reshape(1, cols),
    )
    return (outs[0].reshape(rows), outs[1].reshape(cols), outs[2], outs[3])


def solution(mesh):
    return jax.shard_map(
        on_device,
        mesh=mesh,
        in_specs=(P("wide", None), P("narrow", None), P("wide"), P("narrow"), P("narrow")),
        out_specs=(P("wide"), P("narrow"), P("wide", None), P(("narrow", "wide"), None)),
        check_vma=False,
    )
```

```python
import functools

import jax
import jax.numpy as jnp
from jax import lax
from jax.experimental import pallas as pl
from jax.experimental.pallas import tpu as pltpu
from jax.sharding import PartitionSpec as P

ITERS = 2
EPS = 0.05
SHIFT = 30.0
CENTRE = 2.0 / EPS
LOG2E = 1.4426950408889634
MESH = pl.DeviceIdType.MESH
NT = (((1,), (1,)), ((), ()))


def unit_of(desc):
    wide32 = desc.astype(jnp.float32)
    total = jnp.sum(wide32 * wide32, axis=1, keepdims=True) + 1e-06
    return (wide32 / jnp.sqrt(total)).astype(jnp.bfloat16)


def scaled_rows(logs, top):
    val = jnp.exp(logs - top + SHIFT)
    high = val.astype(jnp.bfloat16).astype(jnp.float32)
    low = val - high
    row = lax.broadcasted_iota(jnp.int32, (16, logs.shape[1]), 0)
    return val, jnp.where(row == 0, high, jnp.where(row == 1, low, 0.0)).astype(jnp.bfloat16)


def scale_out(log_a, log_b, in_a, in_b, pot_a, pot_b, flow_a, flow_b):
    pot_a[...] = EPS * log_a[...]
    pot_b[...] = EPS * log_b[...]
    flow_a[...] = in_a[...]
    flow_b[...] = in_b[...]


def kernel(
    nw, nn,
    desc_a, desc_b, lm_a, lm_b, g_start,
    pot_a, pot_b, flow_a, flow_b,
    a_in, unit_a, unit_b, a_t, b_t, k_rows, k_cols, rows16, weighted,
    phi_in, psi_in, lse_in, flow_in, l_row, t_row, fsum,
    a_send, a_recv, phi_send, phi_recv, psi_send, psi_recv, lse_send, lse_recv, f_send, f_recv,
):
    wide = lax.axis_index("wide")
    narrow = lax.axis_index("narrow")
    rows, feat = desc_a.shape
    cols = desc_b.shape[0]
    share = cols // nw
    all_rows = nw * rows
    own_cols = pl.ds(pl.multiple_of(wide * share, share), share)
    own_rows = pl.ds(pl.multiple_of(wide * rows, rows), rows)

    barrier = pltpu.get_barrier_semaphore()
    for k in range(1, nw):
        pl.semaphore_signal(
            barrier, inc=1, device_id={"wide": lax.rem(wide + k, nw)}, device_id_type=MESH
        )
    for k in range(1, nn):
        pl.semaphore_signal(
            barrier, inc=1, device_id={"narrow": lax.rem(narrow + k, nn)}, device_id_type=MESH
        )

    def spread(axis, size, me, src, dst, send, recv):
        copies = []
        for k in range(1, size):
            copy = pltpu.make_async_remote_copy(
                src_ref=src, dst_ref=dst, send_sem=send.at[k], recv_sem=recv.at[k],
                device_id={axis: lax.rem(me + k, size)}, device_id_type=MESH,
            )
            copy.start()
            copies.append(copy)
        return copies

    def finish(copies):
        for copy in copies:
            copy.wait()

    own_unit = unit_of(desc_a[...])
    step_b = min(cols, 512)

    @pl.loop(0, cols // step_b)
    def _(c):
        at = pl.ds(pl.multiple_of(c * step_b, step_b), step_b)
        unit_b[at, :] = unit_of(desc_b[at, :])

    pl.semaphore_wait(barrier, nw + nn - 2)

    half = rows // 2
    side = lax.rem(narrow, 2)
    mine = pl.ds(pl.multiple_of(side * half, half), half)
    inner = lax.rem(wide, 2)
    outer = lax.div(wide, 2)
    n_outer = nw // 2

    def block_of(k, flipped):
        line = 1 - inner if flipped else inner
        return lax.rem(outer - k + n_outer, n_outer) * 2 + line

    def pass_on(src, block, slot, device):
        copy = pltpu.make_async_remote_copy(
            src_ref=src, dst_ref=a_in.at[block, mine], send_sem=a_send.at[slot],
            recv_sem=a_recv.at[slot], device_id=device, device_id_type=MESH,
        )
        copy.start()
        return copy

    def to_line(k):
        return {"wide": lax.rem(outer + k, n_outer) * 2 + inner}

    to_next = {"wide": wide + 1 - 2 * inner}
    to_twin = {"narrow": narrow + 1 - 2 * side}
    along = [pass_on(desc_a.at[mine], wide, k, to_line(k)) for k in range(1, n_outer)]
    across = [pass_on(desc_a.at[mine], wide, n_outer, to_next)]
    twin = []

    chunk = 256

    @pl.loop(0, cols // chunk, unroll=4)
    def _(c):
        at = pl.ds(pl.multiple_of(c * chunk, chunk), chunk)
        dots = lax.dot_general(unit_b[at, :], own_unit, NT, preferred_element_type=jnp.float32)
        k_cols[at, :] = jnp.exp2(dots * (CENTRE * LOG2E)).astype(jnp.bfloat16)

    def log_sums(logs, mat, out):
        top = jnp.max(logs, axis=1, keepdims=True)
        val, pair = scaled_rows(logs, top)
        depth, width = mat.shape
        rows16[:, :depth] = pair
        block = min(width, 256)
        for c in range(width // block):
            at = pl.ds(c * block, block)
            got = jnp.dot(rows16[:, :depth], mat[:, at], preferred_element_type=jnp.float32)
            out[:, at] = jnp.log(got[0:1, :] + got[1:2, :]) + (top - SHIFT - CENTRE)
        return val, top

    def weighted_sums(val, tokens_t, mat, base, top, write):
        depth, width = mat.shape
        step = min(depth, 1024)
        for c in range(depth // step):
            at = pl.ds(c * step, step)
            part = tokens_t[:, at].astype(jnp.float32) * val[:, c * step:(c + 1) * step]
            weighted[:, at] = part.astype(jnp.bfloat16)
        block = min(width, 256)
        for c in range(width // block):
            at = pl.ds(c * block, block)
            got = jnp.dot(weighted[:, :depth], mat[:, at], preferred_element_type=jnp.float32)
            scale = jnp.exp((top - SHIFT - CENTRE) - base[:, at])
            write(at, got * scale)

    def joined(buf, t, n):
        return jnp.concatenate([buf[t, w] for w in range(n)], axis=1)

    def narrow_lse(t):
        parts = [lse_in[t, n] for n in range(nn)]
        top = functools.reduce(jnp.maximum, parts)
        return top + jnp.log(sum(jnp.exp(p - top) for p in parts))

    pending = []
    psi = g_start[...] / EPS
    for t in range(ITERS + 1):
        v_val, v_top = log_sums(psi, k_cols, l_row)
        lse_in[t, narrow] = l_row[...]
        lse_copies = spread(
            "narrow", nn, narrow, lse_in.at[t, narrow], lse_in.at[t, narrow],
            lse_send.at[t], lse_recv.at[t],
        )
        if t == ITERS:
            def put_a(at, value):
                flow_in[narrow, :, at] = value.astype(jnp.bfloat16)

            weighted_sums(v_val, b_t, k_cols, l_row, v_top, put_a)
            f_copies = spread(
                "narrow", nn, narrow, flow_in.at[narrow], flow_in.at[narrow], f_send, f_recv
            )
            finish(lse_copies)
            lse_a = narrow_lse(t)
            pot_a[...] = lm_a[...] - lse_a
            finish(f_copies)
            acc = jnp.zeros((feat, rows), jnp.float32)
            for n in range(nn):
                acc += flow_in[n].astype(jnp.float32) * jnp.exp(lse_in[t, n] - lse_a)
            flow_a[...] = acc.T - own_unit.astype(jnp.float32)
            break
        if t == 0:
            for k in range(1, n_outer):
                along[k - 1].wait_recv()
                block = block_of(k, False)
                src = a_in.at[block, mine]
                across.append(pass_on(src, block, n_outer + k, to_next))
                twin.append(pass_on(src, block, 2 * n_outer + k, to_twin))
        finish(lse_copies)
        phi_in[t, wide] = lm_a[...] - narrow_lse(t)
        phi_copies = spread(
            "wide", nw, wide, phi_in.at[t, wide], phi_in.at[t, wide],
            phi_send.at[t], phi_recv.at[t],
        )
        if t == 0:
            for k in range(n_outer):
                across[k].wait_recv()
                block = block_of(k, True)
                twin.append(pass_on(a_in.at[block, mine], block, 3 * n_outer + k, to_twin))
            for copy in along + across:
                copy.wait_send()
            finish(twin)
            a_in[wide] = desc_a[...]

            for w in range(nw):
                unit_a[pl.ds(w * rows, rows), :] = unit_of(a_in[w])
            own_b = unit_b[own_cols, :]

            @pl.loop(0, all_rows // chunk, unroll=4)
            def _(c):
                at = pl.ds(pl.multiple_of(c * chunk, chunk), chunk)
                dots = lax.dot_general(unit_a[at, :], own_b, NT, preferred_element_type=jnp.float32)
                k_rows[at, :] = jnp.exp2(dots * (CENTRE * LOG2E)).astype(jnp.bfloat16)

        finish(phi_copies)
        phi = joined(phi_in, t, nw)
        u_val, u_top = log_sums(phi, k_rows, t_row)
        psi_in[t, wide] = lm_b[:, own_cols] - t_row[...]
        psi_copies = spread(
            "wide", nw, wide, psi_in.at[t, wide], psi_in.at[t, wide],
            psi_send.at[t], psi_recv.at[t],
        )
        if t == 0:
            @pl.loop(0, cols // step_b)
            def _(c):
                at = pl.ds(pl.multiple_of(c * step_b, step_b), step_b)
                b_t[:, at] = unit_b[at, :].T

            for w in range(nw):
                at = pl.ds(w * rows, rows)
                a_t[:, at] = unit_a[at, :].T
        if t == ITERS - 1:
            def put_b(at, value):
                flow_b[at, :] = value.T - unit_b[
                    pl.ds(pl.multiple_of(wide * share + at.start, 128), at.size), :
                ].astype(jnp.float32)

            weighted_sums(u_val, a_t, k_rows, t_row, u_top, put_b)
        finish(psi_copies)
        psi = joined(psi_in, t, nw)
    pot_b[...] = psi


def on_device(desc_a, desc_b, logmass_a, logmass_b, g_start):
    nw = lax.axis_size("wide")
    nn = lax.axis_size("narrow")
    rows, feat = desc_a.shape
    cols = desc_b.shape[0]
    share = cols // nw
    all_rows = nw * rows
    longest = max(all_rows, cols)
    f32, bf16 = jnp.float32, jnp.bfloat16
    vmem = pltpu.VMEM
    dma = pltpu.SemaphoreType.DMA
    outs = pl.pallas_call(
        functools.partial(kernel, nw, nn),
        out_shape=(
            jax.ShapeDtypeStruct((1, rows), f32),
            jax.ShapeDtypeStruct((1, cols), f32),
            jax.ShapeDtypeStruct((rows, feat), f32),
            jax.ShapeDtypeStruct((share, feat), f32),
        ),
        in_specs=[pl.BlockSpec(memory_space=vmem)] * 5,
        out_specs=(pl.BlockSpec(memory_space=vmem),) * 4,
        scratch_shapes=[
            vmem((nw, rows, feat), bf16),
            vmem((all_rows, feat), bf16),
            vmem((cols, feat), bf16),
            vmem((feat, all_rows), bf16),
            vmem((feat, cols), bf16),
            vmem((all_rows, share), bf16),
            vmem((cols, rows), bf16),
            vmem((16, longest), bf16),
            vmem((feat, longest), bf16),
            vmem((ITERS, nw, 1, rows), f32),
            vmem((ITERS, nw, 1, share), f32),
            vmem((ITERS + 1, nn, 1, rows), f32),
            vmem((nn, feat, rows), bf16),
            vmem((1, rows), f32),
            vmem((1, share), f32),
            vmem((8, 128), f32),
            dma((2 * nw,)), dma((2 * nw,)),
            dma((ITERS, nw)), dma((ITERS, nw)),
            dma((ITERS, nw)), dma((ITERS, nw)),
            dma((ITERS + 1, nn)), dma((ITERS + 1, nn)),
            dma((nn,)), dma((nn,)),
        ],
        compiler_params=pltpu.CompilerParams(
            collective_id=0, has_side_effects=True, vmem_limit_bytes=60 * 1024 * 1024
        ),
        name="sinkhorn",
    )(
        desc_a, desc_b, logmass_a.reshape(1, rows), logmass_b.reshape(1, cols),
        g_start.reshape(1, cols),
    )
    outs = pl.pallas_call(
        scale_out,
        out_shape=tuple(jax.ShapeDtypeStruct(o.shape, f32) for o in outs),
        in_specs=[pl.BlockSpec(memory_space=vmem)] * 4,
        out_specs=(pl.BlockSpec(memory_space=vmem),) * 4,
        name="scale_out",
    )(*outs)
    return (outs[0].reshape(rows), outs[1].reshape(cols), outs[2], outs[3])


def solution(mesh):
    return jax.shard_map(
        on_device,
        mesh=mesh,
        in_specs=(P("wide", None), P("narrow", None), P("wide"), P("narrow"), P("narrow")),
        out_specs=(P("wide"), P("narrow"), P("wide", None), P(("narrow", "wide"), None)),
        check_vma=False,
    )
```
